1024 devices in a mesh: dp: 4 (over z_lo), expert: 32 (over z_hi, x, core), tensor: 8 (over y).
Axes of the slice: x: 8, y: 8, z: 8 (z_hi: 2, z_lo: 4; z = z_hi * 4 + z_lo), core: 2. Of those that a mesh axis runs over, the one named last changes fastest.
Arguments:
- tokens: bfloat16 [16384, 2048], P(('dp', 'expert')), may hold values from -6 to 6
- cotangent: bfloat16 [16384, 2048], P(('dp', 'expert')), may hold values from -6 to 6
- scores: float32 [16384, 8], P(('dp', 'expert')), may hold values from 0.05 to 1
- routes: int32 [16384, 1], P(('dp', 'expert')), may hold values from 0 to 63; in each aligned block of 128 rows (0 to 127, 128 to 255, ...) at most 4 rows name the same one
- w_gate: bfloat16 [64, 2048, 768], P('expert', 'dp', 'tensor'), may hold values from -0.125 to 0.125
- w_up: bfloat16 [64, 2048, 768], P('expert', 'dp', 'tensor'), may hold values from -0.125 to 0.125
- w_down: bfloat16 [64, 768, 2048], P('expert', 'tensor', 'dp'), may hold values from -0.21875 to 0.21875
Outputs:
- output: bfloat16 [16384, 2048], P(('dp', 'expert'), 'tensor')
- grad_tokens: bfloat16 [16384, 2048], P(('dp', 'expert'), 'tensor')
- grad_gate: float32 [64, 2048, 768], P('expert', 'dp', 'tensor')
- grad_up: float32 [64, 2048, 768], P('expert', 'dp', 'tensor')
- grad_down: float32 [64, 768, 2048], P('expert', 'tensor', 'dp')
The draws below stay inside these ranges and needn't reach their ends.
Inputs may be any that keep to these rules, and one draw needn't show every extreme that they name: `routes`: each row names 1 different experts. Among the rows of one token block no expert is named more than 4 times, and 4 is reached.
All inputs are finite; a program needn't handle non-finite values.
Results may differ from the reference program's by a relative error of at most 0.019.
Values may be sent and summed in bfloat16 or wider, within the bound.
A program may use at most 32 MiB of HBM per device.

```python
import math
import jax
import jax.numpy as jnp
import numpy as np
from jax import lax

D = 2048
FF = 768
TOP = 8
FLIGHT = 1
TOK_DEV = 128
EXPERTS = 64
TOKEN_GROUPS = 4
SOURCES = 32
UNIT_GROUPS = 8
SHARE = 96
CAP = 4
TOKENS = 16384


def steps_of(key, shape, split, low, high):
    level = 1.0
    for dim, parts in split:
        heights = jax.random.uniform(jax.random.fold_in(jax.random.fold_in(key, 6), dim), (parts,), jnp.float32, low / len(split), high / len(split))
        level = level * jnp.repeat(jnp.exp(heights), shape[dim] // parts).reshape((-1,) + (1,) * (len(shape) - 1 - dim))
    return level


def deal_out(rng, own, number, rows, amount, top, most, lean):
    sequence = jax.random.permutation(rng, amount)
    heavy_load, usual = portions_of(amount, rows * top, most, lean, True), portions_of(amount, rows * top, most, lean, False)
    places = jnp.arange(amount)

    def named(lengths, rotation):
        used = int((lengths > 0).sum())
        fixed = max(1, used // 4)
        moved = fixed + (places - fixed + rotation * (used - fixed)) % max(1, amount - fixed)
        return jnp.zeros((amount,), jnp.int32).at[sequence[jnp.where(places < fixed, places, moved)]].set(jnp.asarray(lengths, jnp.int32))

    lengths = jnp.where(number % 4 == 0, named(heavy_load, number // 4), named(usual, number - number // 4 - 1))
    mixed = jax.random.permutation(jax.random.fold_in(own, 3), amount)
    giver, taker = mixed[0:amount // 2 * 2:2], mixed[1:amount // 2 * 2:2]
    room = jnp.minimum(lengths[giver] - 1, most - lengths[taker]) // 2
    room = jnp.where((giver == sequence[0]) | (taker == sequence[0]) | (lengths[taker] == 0), 0, jnp.maximum(room, 0))
    moved = jax.random.randint(jax.random.fold_in(own, 4), (amount // 2,), 0, 1 << 20) % (room + 1)
    lengths = lengths.at[giver].add(-moved).at[taker].add(moved)
    members = jnp.searchsorted(jnp.cumsum(lengths), jnp.arange(rows * top), side="right").astype(jnp.int32)
    grid = members.reshape(top, rows).T
    grid = grid[jax.random.permutation(jax.random.fold_in(own, 1), rows)]
    rotation = jax.random.randint(jax.random.fold_in(own, 2), (rows, 1), 0, top)
    return jnp.take_along_axis(grid, (jnp.arange(top)[None, :] + rotation) % top, axis=1)


def portions_of(amount, total, bound, skew, full):
    weights = [(1 << 20) // math.isqrt(standing ** skew) + 1 for standing in range(1, amount + 1)]
    largest = bound if full else min(bound, max(-(-total // amount), total * weights[0] // sum(weights)))
    least = 1 if total - largest >= amount - 1 else 0
    counts, spare = [largest] + [least] * (amount - 1), total - largest - least * (amount - 1)
    while spare > 0:
        candidates = [i for i in range(1, amount) if counts[i] < largest] or [i for i in range(1, amount) if counts[i] < bound]
        mass, remaining = sum([weights[i] for i in candidates]), spare
        for i in candidates:
            more = min(bound - counts[i], max(1, remaining * weights[i] // mass), spare)
            counts[i] = counts[i] + more
            spare = spare - more
    return np.array(counts)


def noise(rng, shape, scale, limit, split=(), kind=jnp.bfloat16):
    array = scale * jax.random.normal(rng, shape, jnp.float32)
    if split:
        array = array * steps_of(rng, shape, split, -0.22, 0.18)
    return jnp.clip(array, -limit, limit).astype(kind)


def setup_inputs(seed: int = 0) -> dict:
    keys = jax.random.split(jax.random.key(seed), 8)
    tokens = noise(keys[0], (TOKENS, D), 1.0, 6.0, ((0, 128),))
    cotangent = noise(keys[1], (TOKENS, D), 1.0, 6.0, ((0, 128),))
    scores = jnp.clip(jnp.exp(math.log(1.0) - 2.9957323 * jax.random.uniform(keys[2], (TOKENS, TOP), jnp.float32) ** steps_of(keys[2], (TOKENS, TOP), ((0, 128),), -0.2, 0.2)), 0.05, 1.0)
    routes_keys = jax.random.split(jax.random.fold_in(keys[3], 1), TOKENS // TOK_DEV)
    routes_turns = jax.random.permutation(jax.random.fold_in(keys[3], 3), TOKENS // TOK_DEV)
    routes = jax.vmap(lambda own, number: deal_out(jax.random.fold_in(keys[3], 2), own, number, TOK_DEV, EXPERTS, FLIGHT, CAP, 2))(routes_keys, routes_turns).reshape((TOKENS, FLIGHT))
    w_gate = noise(keys[4], (EXPERTS, D, FF), D ** -0.5, 0.125, ((0, 32), (1, 4), (2, 8)))
    w_up = noise(keys[5], (EXPERTS, D, FF), D ** -0.5, 0.125, ((0, 32), (1, 4), (2, 8)))
    w_down = noise(keys[6], (EXPERTS, FF, D), FF ** -0.5, 0.21875, ((0, 32), (1, 8), (2, 4)))
    return dict(tokens=tokens, cotangent=cotangent, scores=scores, routes=routes, w_gate=w_gate, w_up=w_up, w_down=w_down)


def rounded(value):
    return lax.optimization_barrier(value.astype(jnp.bfloat16)).astype(jnp.float32)


def slot_onehot(route_block, expert_count, capacity):
    flat = route_block.reshape(-1).astype(jnp.int32)
    member = (flat[:, None] == jnp.arange(expert_count, dtype=jnp.int32)[None, :]).astype(jnp.int32)
    before = jnp.cumsum(member, axis=0) - member
    place = jnp.sum(before * member, axis=1)
    slot_ids = flat * capacity + place
    return slot_ids[:, None] == jnp.arange(expert_count * capacity, dtype=jnp.int32)[None, :]


def reference(tokens, cotangent, scores, routes, w_gate, w_up, w_down):
    highest = lax.Precision.HIGHEST
    owners = SOURCES
    slots = EXPERTS * CAP
    gate_full = w_gate.astype(jnp.float32)
    up_full = w_up.astype(jnp.float32)
    down_full = w_down.astype(jnp.float32)
    sum_gate = jnp.zeros((EXPERTS, D, FF), jnp.float32)
    sum_up = jnp.zeros((EXPERTS, D, FF), jnp.float32)
    sum_down = jnp.zeros((EXPERTS, FF, D), jnp.float32)
    outs_y = []
    outs_x = []
    span = owners * TOK_DEV
    for group in range(TOKEN_GROUPS):
        rows_in = tokens[group * span:(group + 1) * span].reshape(owners, TOK_DEV, D)
        rows_cot = cotangent[group * span:(group + 1) * span].reshape(owners, TOK_DEV, D)
        block_scores = scores[group * span:(group + 1) * span].reshape(owners, TOK_DEV, TOP)
        block_routes = routes[group * span:(group + 1) * span].reshape(owners, TOK_DEV, FLIGHT)
        table = jax.vmap(lambda one: slot_onehot(one, EXPERTS, CAP))(block_routes).astype(jnp.float32)
        mix = (block_scores / jnp.sum(block_scores, axis=2, keepdims=True))[:, :, :FLIGHT]
        rep_x = jnp.repeat(rows_in.astype(jnp.float32), FLIGHT, axis=1)
        rep_d = rounded(mix[:, :, :, None] * rows_cot.astype(jnp.float32)[:, :, None, :]).reshape(owners, TOK_DEV * FLIGHT, D)
        send_x = jnp.einsum('nrs,nrd->nsd', table, rep_x, precision=highest)
        send_d = jnp.einsum('nrs,nrd->nsd', table, rep_d, precision=highest)
        x_rows = send_x.reshape(owners, EXPERTS, CAP, D).transpose(1, 0, 2, 3).reshape(EXPERTS, owners * CAP, D)
        d_rows = send_d.reshape(owners, EXPERTS, CAP, D).transpose(1, 0, 2, 3).reshape(EXPERTS, owners * CAP, D)
        gate_act = jnp.einsum('erd,edf->erf', x_rows, gate_full, precision=highest)
        up_act = jnp.einsum('erd,edf->erf', x_rows, up_full, precision=highest)
        sigma = jax.nn.sigmoid(gate_act)
        silu_act = gate_act * sigma
        hidden = rounded(silu_act * up_act)
        back_grad = jnp.einsum('erd,efd->erf', d_rows, down_full, precision=highest)
        grad_act_gate = rounded(back_grad * up_act * sigma * (1.0 + gate_act * (1.0 - sigma)))
        grad_act_up = rounded(back_grad * silu_act)
        out_rows = jnp.zeros((EXPERTS, owners * CAP, D), jnp.float32)
        in_rows = jnp.zeros((EXPERTS, owners * CAP, D), jnp.float32)
        for unit in range(UNIT_GROUPS):
            lo = unit * SHARE
            hi = lo + SHARE
            out_rows = out_rows + rounded(jnp.einsum('erf,efd->erd', hidden[:, :, lo:hi], down_full[:, lo:hi, :], precision=highest))
            in_term = jnp.einsum('erf,edf->erd', grad_act_gate[:, :, lo:hi], gate_full[:, :, lo:hi], precision=highest)
            in_term = in_term + jnp.einsum('erf,edf->erd', grad_act_up[:, :, lo:hi], up_full[:, :, lo:hi], precision=highest)
            in_rows = in_rows + rounded(in_term)
        back_y = out_rows.reshape(EXPERTS, owners, CAP, D).transpose(1, 0, 2, 3).reshape(owners, slots, D)
        back_x = in_rows.reshape(EXPERTS, owners, CAP, D).transpose(1, 0, 2, 3).reshape(owners, slots, D)
        spread = table.reshape(owners, TOK_DEV, FLIGHT, slots)
        weighted = jnp.einsum('ntks,ntk->nts', spread, mix, precision=highest)
        plain = jnp.sum(spread, axis=2)
        outs_y.append(jnp.einsum('nts,nsd->ntd', weighted, back_y, precision=highest))
        outs_x.append(jnp.einsum('nts,nsd->ntd', plain, back_x, precision=highest))
        sum_gate = sum_gate + rounded(jnp.einsum('erd,erf->edf', x_rows, grad_act_gate, precision=highest))
        sum_up = sum_up + rounded(jnp.einsum('erd,erf->edf', x_rows, grad_act_up, precision=highest))
        sum_down = sum_down + rounded(jnp.einsum('erf,erd->efd', hidden, d_rows, precision=highest))
    output = jnp.concatenate(outs_y, axis=0).reshape(TOKENS, D).astype(jnp.bfloat16)
    grad_tokens = jnp.concatenate(outs_x, axis=0).reshape(TOKENS, D).astype(jnp.bfloat16)
    return output, grad_tokens, sum_gate, sum_up, sum_down
```

```python
import functools

import jax
import jax.numpy as jnp
from jax import lax
from jax.experimental import pallas as pl
from jax.experimental.pallas import tpu as pltpu
from jax.sharding import PartitionSpec as P

MESH = pl.DeviceIdType.MESH
F32 = jnp.float32
BF16 = jnp.bfloat16
CAP = 4
LANES = 128
NT = (((1,), (1,)), ((), ()))
TN = (((0,), (0,)), ((), ()))


def dot(a, b, dims=(((1,), (0,)), ((), ()))):
    return lax.dot_general(a, b, dims, preferred_element_type=F32)


def kernel(
    cfg,
    tok, cot, sco, rou, wg, wu, wd,
    out, gtk, gg, gu, gd,
    sb, xb, wgu, wdn, pf, ps, pr, hb, ga2, hid2, part, ss, rv, fin, rb, slots,
    dsp_s, dsp_r, ag_s, ag_r, b_s, b_r, c_s, c_r, rs_s, rs_r, rt_s, rt_r,
):
    ZL, ZH, X, C, Y = cfg
    J = ZL * ZH * C
    R = J * 8
    GR = ZH * C * 8
    HALF = R // 2
    S = Y // 2
    HN = Y // ZL
    NE = ZH * X * C
    T = tok.shape[0]
    DS = wg.shape[1]
    FS = wg.shape[2]
    CW = out.shape[1]

    d = lax.axis_index("dp")
    e = lax.axis_index("expert")
    t = lax.axis_index("tensor")
    zh = e // (X * C)
    x = (e // C) % X
    c = e % C
    hop = (Y // 2) * zh + (Y // 4) * c
    jme = d * (ZH * C) + zh * C + c
    right = (d, e, (t + 1) % Y)
    left = (d, e, (t + Y - 1) % Y)

    def peer(j):
        zl_p = j // (ZH * C)
        zh_p = (j // C) % ZH
        c_p = j % C
        x_p = (t + 8 * Y - x - hop - (Y // 2) * zh_p - (Y // 4) * c_p) % X
        e_p = zh_p * (X * C) + x_p * C + c_p
        return zl_p, e_p

    def same(zl_p, e_p, t_p):
        return jnp.logical_and(jnp.logical_and(zl_p == d, e_p == e), t_p == t)

    barrier = pltpu.get_barrier_semaphore()

    def greet(zl_p, e_p, t_p):
        me = same(zl_p, e_p, t_p)

        @pl.when(jnp.logical_not(me))
        def _():
            pl.semaphore_signal(barrier, inc=1, device_id=(zl_p, e_p, t_p), device_id_type=MESH)

        return jnp.where(me, 0, 1)

    def greet_dispatch(j, n):
        zl_p, e_p = peer(j)
        return n + greet(zl_p, e_p, t)

    def greet_return(i, n):
        zl_p = t // HN
        hop_p = (Y // 2) * (i // (X * C)) + (Y // 4) * (i % C)
        return n + greet(zl_p, i, (x + hop + (i // C) % X + hop_p) % Y)

    count = lax.fori_loop(0, J, greet_dispatch, jnp.int32(0))
    count = lax.fori_loop(0, NE, greet_return, count)
    for dev in (right, left):
        pl.semaphore_signal(barrier, inc=1, device_id=dev, device_id_type=MESH)
    for o in range(1, ZL):
        pl.semaphore_signal(barrier, inc=1, device_id=((d + o) % ZL, e, t), device_id_type=MESH)

    sub = lax.broadcasted_iota(jnp.int32, (T, T), 0)
    lan = lax.broadcasted_iota(jnp.int32, (T, T), 1)
    rcol = rou[...]
    rrow = jnp.sum(jnp.where(sub == lan, rcol, 0), axis=0, keepdims=True)
    place = jnp.sum(jnp.where((rcol == rrow) & (lan < sub), 1, 0), axis=1, keepdims=True)
    scol = rcol * CAP + place
    slots[...] = scol
    srow = jnp.sum(jnp.where(sub == lan, scol, 0), axis=0, keepdims=True)
    row = lax.broadcasted_iota(jnp.int32, (R, T), 0)
    jv = row // 8
    zh_v = (jv // C) % ZH
    c_v = jv % C
    x_v = (t + 8 * Y - x - hop - (Y // 2) * zh_v - (Y // 4) * c_v) % X
    want = (zh_v * (X * C) + x_v * C + c_v) * 8 + row % 8
    pick = jnp.where(want == srow, 1.0, 0.0).astype(BF16)
    scores = sco[...]
    mix = scores[:, 0:1] / jnp.sum(scores, axis=1, keepdims=True)
    for g in range(ZL):
        cols = slice(g * DS, (g + 1) * DS)
        rows = slice(g * GR, (g + 1) * GR)
        sb[rows, 0:DS] = dot(pick[rows], tok[:, cols]).astype(BF16)
        dg = (mix * cot[:, cols].astype(F32)).astype(BF16)
        sb[rows, DS : 2 * DS] = dot(pick[rows], dg).astype(BF16)

    pl.semaphore_wait(barrier, count + 2 + ZL - 1)

    def dsp_copy(j, zl_p, e_p, slot):
        return pltpu.make_async_remote_copy(
            src_ref=sb.at[pl.ds(pl.multiple_of(j * 8, 8), 8), :],
            dst_ref=xb.at[0, pl.ds(pl.multiple_of(slot * 8, 8), 8), :],
            send_sem=dsp_s.at[j],
            recv_sem=dsp_r.at[slot],
            device_id=(zl_p, e_p, t),
            device_id_type=MESH,
        )

    def dsp_local(j):
        rows = pl.ds(pl.multiple_of(j * 8, 8), 8)
        return pltpu.make_async_copy(sb.at[rows, :], xb.at[0, rows, :], dsp_r.at[j])

    def dsp_start(j, carry):
        zl_p, e_p = peer(j)
        me = same(zl_p, e_p, t)

        @pl.when(me)
        def _():
            dsp_local(j).start()

        @pl.when(jnp.logical_not(me))
        def _():
            dsp_copy(j, zl_p, e_p, jme).start()

        return carry

    lax.fori_loop(0, J, dsp_start, 0)

    wgu[...] = jnp.zeros_like(wgu)
    wdn[...] = jnp.zeros_like(wdn)
    for n in range(2):
        wgu[:, n * LANES : n * LANES + FS] = wg[n]
        wgu[:, (2 + n) * LANES : (2 + n) * LANES + FS] = wu[n]
        wdn[n * LANES : n * LANES + FS, :] = wd[n]
    first = lax.broadcasted_iota(jnp.int32, (R, LANES), 0) % 8 < CAP
    m0 = jnp.where(first, 1.0, 0.0).astype(BF16)
    m1 = jnp.where(first, 0.0, 1.0).astype(BF16)

    def dsp_wait(j, carry):
        dsp_local(j).wait()
        return carry

    lax.fori_loop(0, J, dsp_wait, 0)

    def ag_copy(way, s, hf):
        src = (-s) % Y if way == 0 else s
        dst = (-s - 1) % Y if way == 0 else s + 1
        rows = pl.ds(hf * HALF, HALF)
        return pltpu.make_async_remote_copy(
            src_ref=xb.at[src, rows, :],
            dst_ref=xb.at[dst, rows, :],
            send_sem=ag_s.at[way, s, hf],
            recv_sem=ag_r.at[way, s, hf],
            device_id=right if way == 0 else left,
            device_id_type=MESH,
        )

    def ag_live(way, s, hf):
        return s < S - 1 or hf == way

    def ag_start(s, way, hf):
        if s < S and ag_live(way, s, hf):
            ag_copy(way, s, hf).start()

    def b_copy(k, o):
        g = (d + o) % ZL
        return pltpu.make_async_remote_copy(
            src_ref=ps.at[k, g],
            dst_ref=pr.at[k, o - 1],
            send_sem=b_s.at[k, o - 1],
            recv_sem=b_r.at[k, o - 1],
            device_id=(g, e, t),
            device_id_type=MESH,
        )

    def c_copy(k, o):
        return pltpu.make_async_remote_copy(
            src_ref=hb.at[k, d],
            dst_ref=hb.at[k, d],
            send_sem=c_s.at[k, o - 1],
            recv_sem=c_r.at[k, o - 1],
            device_id=((d + o) % ZL, e, t),
            device_id_type=MESH,
        )

    def partial(k):
        xg = dot(xb[k, :, 0:DS], wgu[...])
        bk = dot(xb[k, :, DS : 2 * DS], wdn[...], NT)
        sel = [
            jnp.where(first, xg[:, 0:LANES], xg[:, LANES : 2 * LANES]),
            jnp.where(first, xg[:, 2 * LANES : 3 * LANES], xg[:, 3 * LANES : 4 * LANES]),
            jnp.where(first, bk[:, 0:LANES], bk[:, LANES : 2 * LANES]),
        ]
        for n in range(3):
            cols = slice(n * LANES, (n + 1) * LANES)
            val = sel[n].reshape(ZL, GR, LANES)
            pf[k, :, :, cols] = val
            ps[k, :, :, cols] = val.astype(BF16)
        for o in range(1, ZL):
            b_copy(k, o).start()

    def activate(k):
        for o in range(1, ZL):
            b_copy(k, o).wait_recv()
        acts = pf[k, d]
        for o in range(1, ZL):
            acts = acts + pr[k, o - 1].astype(F32)
        gate = acts[:, 0:LANES]
        up = acts[:, LANES : 2 * LANES]
        back = acts[:, 2 * LANES : 3 * LANES]
        sig = jax.nn.sigmoid(gate)
        silu = gate * sig
        hb[k, d, :, 0:LANES] = (silu * up).astype(BF16)
        hb[k, d, :, LANES : 2 * LANES] = (back * up * sig * (1.0 + gate * (1.0 - sig))).astype(BF16)
        hb[k, d, :, 2 * LANES : 3 * LANES] = (back * silu).astype(BF16)
        for o in range(1, ZL):
            c_copy(k, o).start()

    def c_wait(k):
        for o in range(1, ZL):
            g = (d + ZL - o) % ZL
            pltpu.make_async_remote_copy(
                src_ref=hb.at[k, g],
                dst_ref=hb.at[k, g],
                send_sem=c_s.at[k, o - 1],
                recv_sem=c_r.at[k, o - 1],
                device_id=((d + o) % ZL, e, t),
                device_id_type=MESH,
            ).wait_recv()

    def finish(k):
        c_wait(k)
        acts = hb[k].reshape(R, 3 * LANES)
        hid = acts[:, 0:LANES]
        hid2[k, :, 0:LANES] = hid * m0
        hid2[k, :, LANES : 2 * LANES] = hid * m1
        for n in range(2):
            ga = acts[:, (1 + n) * LANES : (2 + n) * LANES]
            ga2[k, :, 2 * n * LANES : (2 * n + 1) * LANES] = ga * m0
            ga2[k, :, (2 * n + 1) * LANES : (2 * n + 2) * LANES] = ga * m1
        part[k, :, 0:DS] = dot(hid2[k], wdn[...])
        part[k, :, DS : 2 * DS] = dot(ga2[k], wgu[...], NT)

    for hf in range(2):
        for way in range(2):
            ag_start(0, way, hf)
    partial(0)
    late = [0]
    for s in range(S):
        for hf in range(2):
            for way in range(2):
                if ag_live(way, s, hf):
                    ag_copy(way, s, hf).wait_recv()
                    ag_start(s + 1, way, hf)
        fresh = sorted({(-s - 1) % Y, s + 1})
        for k in fresh:
            partial(k)
        for k in late:
            activate(k)
        late = fresh
    for k in late:
        activate(k)

    def rs_copy(way, s, ch):
        cols = pl.ds(ch * DS, DS)
        return pltpu.make_async_remote_copy(
            src_ref=ss.at[way, s, :, cols],
            dst_ref=rv.at[way, s, :, cols],
            send_sem=rs_s.at[way, s, ch],
            recv_sem=rs_r.at[way, s, ch],
            device_id=right if way == 0 else left,
            device_id_type=MESH,
        )

    def rs_live(way, s, ch):
        return s > 0 or ch == way

    def rs_send(way, s, ch):
        if not rs_live(way, s, ch):
            return
        k = S - s if way == 0 else (s - S) % Y
        cols = slice(ch * DS, (ch + 1) * DS)
        val = part[k, :, cols]
        if s > 0 and rs_live(way, s - 1, ch):
            rs_copy(way, s - 1, ch).wait_recv()
            val = val + rv[way, s - 1, :, cols].astype(F32)
        ss[way, s, :, cols] = val.astype(BF16)
        rs_copy(way, s, ch).start()

    def grads():
        xs = xb[:, :, 0:DS].reshape(Y * R, DS)
        ggu = dot(xs, ga2[...].reshape(Y * R, 4 * LANES), TN)
        for n in range(2):
            gg[n] = ggu[:, n * LANES : n * LANES + FS]
            gu[n] = ggu[:, (2 + n) * LANES : (2 + n) * LANES + FS]
        ds_ = xb[:, :, DS : 2 * DS].reshape(Y * R, DS)
        gdn = dot(hid2[...].reshape(Y * R, 2 * LANES), ds_, TN)
        for n in range(2):
            gd[n] = gdn[n * LANES : n * LANES + FS]

    finish(S)
    rs_send(0, 0, 0)
    rs_send(1, 0, 1)
    for k in range(S - 1, 0, -1):
        finish(k)
        finish(Y - k)
    finish(0)
    for s in range(1, S):
        order = [(0, 0), (1, 1), (0, 1), (1, 0)] if s > 1 else [(0, 1), (1, 0), (0, 0), (1, 1)]
        for way, ch in order:
            rs_send(way, s, ch)
        if s == 1:
            grads()
    if S == 1:
        grads()

    for ch in range(2):
        cols = slice(ch * DS, (ch + 1) * DS)
        val = part[0, :, cols]
        for way in range(2):
            if rs_live(way, S - 1, ch):
                rs_copy(way, S - 1, ch).wait_recv()
                val = val + rv[way, S - 1, :, cols].astype(F32)
        val = val.astype(BF16)
        for h in range(HN):
            fin[h, :, ch * CW : (ch + 1) * CW] = val[:, h * CW : (h + 1) * CW]

    def rt_copy(i, zl_p, e_p, t_p):
        j = i // HN
        return pltpu.make_async_remote_copy(
            src_ref=fin.at[i % HN, pl.ds(pl.multiple_of(j * 8, 8), 8), :],
            dst_ref=rb.at[pl.ds(pl.multiple_of(e * 8, 8), 8), :],
            send_sem=rt_s.at[i],
            recv_sem=rt_r.at[e],
            device_id=(zl_p, e_p, t_p),
            device_id_type=MESH,
        )

    def rt_local(h, j, slot):
        return pltpu.make_async_copy(
            fin.at[h, pl.ds(pl.multiple_of(j * 8, 8), 8), :],
            rb.at[pl.ds(pl.multiple_of(slot * 8, 8), 8), :],
            rt_r.at[slot],
        )

    def rt_start(i, carry):
        zl_p, e_p = peer(i // HN)
        t_p = HN * d + i % HN
        me = same(zl_p, e_p, t_p)

        @pl.when(me)
        def _():
            rt_local(i % HN, i // HN, e).start()

        @pl.when(jnp.logical_not(me))
        def _():
            rt_copy(i, zl_p, e_p, t_p).start()

        return carry

    lax.fori_loop(0, J * HN, rt_start, 0)

    def rt_wait(i, carry):
        rt_local(0, 0, i).wait()
        return carry

    lax.fori_loop(0, NE, rt_wait, 0)

    slot_lane = lax.broadcasted_iota(jnp.int32, (T, NE * 8), 1)
    take = jnp.where(slots[...] == slot_lane, 1.0, 0.0).astype(BF16)
    res = dot(take, rb[...])
    scores = sco[...]
    mix = scores[:, 0:1] / jnp.sum(scores, axis=1, keepdims=True)
    out[...] = (mix * res[:, 0:CW]).astype(BF16)
    gtk[...] = res[:, CW : 2 * CW].astype(BF16)

    def dsp_done(j, carry):
        zl_p, e_p = peer(j)

        @pl.when(jnp.logical_not(same(zl_p, e_p, t)))
        def _():
            dsp_copy(j, zl_p, e_p, jme).wait_send()

        return carry

    lax.fori_loop(0, J, dsp_done, 0)
    for s in range(S):
        for way in range(2):
            for ch in range(2):
                if ag_live(way, s, ch):
                    ag_copy(way, s, ch).wait_send()
                if rs_live(way, s, ch):
                    rs_copy(way, s, ch).wait_send()
    for k in range(Y):
        for o in range(1, ZL):
            b_copy(k, o).wait_send()
            c_copy(k, o).wait_send()

    def rt_done(i, carry):
        zl_p, e_p = peer(i // HN)
        t_p = HN * d + i % HN

        @pl.when(jnp.logical_not(same(zl_p, e_p, t_p)))
        def _():
            rt_copy(i, zl_p, e_p, t_p).wait_send()

        return carry

    lax.fori_loop(0, J * HN, rt_done, 0)


def on_device(cfg, tokens, cotangent, scores, routes, w_gate, w_up, w_down):
    ZL, ZH, X, C, Y = cfg
    J = ZL * ZH * C
    R = J * 8
    GR = ZH * C * 8
    S = Y // 2
    HN = Y // ZL
    NE = ZH * X * C
    T, D = tokens.shape
    _, DS, FS = w_gate.shape
    CW = D // Y
    L3 = 3 * LANES
    vm = pl.BlockSpec(memory_space=pltpu.VMEM)
    dma = pltpu.SemaphoreType.DMA
    return pl.pallas_call(
        functools.partial(kernel, cfg),
        out_shape=(
            jax.ShapeDtypeStruct((T, CW), BF16),
            jax.ShapeDtypeStruct((T, CW), BF16),
            jax.ShapeDtypeStruct(w_gate.shape, F32),
            jax.ShapeDtypeStruct(w_up.shape, F32),
            jax.ShapeDtypeStruct(w_down.shape, F32),
        ),
        in_specs=[vm] * 7,
        out_specs=(vm,) * 5,
        scratch_shapes=[
            pltpu.VMEM((R, 2 * DS), BF16),
            pltpu.VMEM((Y, R, 2 * DS), BF16),
            pltpu.VMEM((DS, 4 * LANES), BF16),
            pltpu.VMEM((2 * LANES, DS), BF16),
            pltpu.VMEM((Y, ZL, GR, L3), F32),
            pltpu.VMEM((Y, ZL, GR, L3), BF16),
            pltpu.VMEM((Y, ZL - 1, GR, L3), BF16),
            pltpu.VMEM((Y, ZL, GR, L3), BF16),
            pltpu.VMEM((Y, R, 4 * LANES), BF16),
            pltpu.VMEM((Y, R, 2 * LANES), BF16),
            pltpu.VMEM((Y, R, 2 * DS), F32),
            pltpu.VMEM((2, S, R, 2 * DS), BF16),
            pltpu.VMEM((2, S, R, 2 * DS), BF16),
            pltpu.VMEM((HN, R, 2 * CW), BF16),
            pltpu.VMEM((NE * 8, 2 * CW), BF16),
            pltpu.VMEM((T, 1), jnp.int32),
            dma((J,)),
            dma((J,)),
            dma((2, S, 2)),
            dma((2, S, 2)),
            dma((Y, ZL - 1)),
            dma((Y, ZL - 1)),
            dma((Y, ZL - 1)),
            dma((Y, ZL - 1)),
            dma((2, S, 2)),
            dma((2, S, 2)),
            dma((J * HN,)),
            dma((NE,)),
        ],
        compiler_params=pltpu.CompilerParams(
            collective_id=0, has_side_effects=True, vmem_limit_bytes=60 * 1024 * 1024
        ),
        name="expert_layer",
    )(tokens, cotangent, scores, routes, w_gate, w_up, w_down)


def solution(mesh, cfg=(4, 2, 8, 2, 8)):
    in_specs = (
        P(("dp", "expert"), None),
        P(("dp", "expert"), None),
        P(("dp", "expert"), None),
        P(("dp", "expert"), None),
        P("expert", "dp", "tensor"),
        P("expert", "dp", "tensor"),
        P("expert", "tensor", "dp"),
    )
    out_specs = (
        P(("dp", "expert"), "tensor"),
        P(("dp", "expert"), "tensor"),
        P("expert", "dp", "tensor"),
        P("expert", "dp", "tensor"),
        P("expert", "tensor", "dp"),
    )
    return jax.shard_map(
        functools.partial(on_device, cfg),
        mesh=mesh,
        in_specs=in_specs,
        out_specs=out_specs,
        check_vma=False,
    )
```
